32 devices in a mesh: seq: 8 (over z, x), tensor: 4 (over y, core).
Axes of the slice: x: 2, y: 2, z: 4, core: 2. Of those that a mesh axis runs over, the one named last changes fastest.
Arguments:
- resid: bfloat16 [1024, 4096], P('seq', 'tensor'), may hold values from -40 to 40
- queries: bfloat16 [1024, 4096], P('seq', 'tensor'), may hold values from -8 to 8
- keys: bfloat16 [1024, 4096], P('seq', 'tensor'), may hold values from -6 to 6
- values: bfloat16 [1024, 4096], P('seq', 'tensor'), may hold values from -18 to 18
- doc_ids: int32 [1024], P('seq'), may hold values from 0 to 3, never falling along the last dimension, each value on 1 to 512 neighbouring positions
- modality: int32 [1024], P('seq'), may hold values from 0 to 2, as said below
- norm_gain: float32 [3, 4096], P(None, 'tensor'), may hold values from 0.1 to 1.9
- gate_w: bfloat16 [4096, 3, 11008], P('tensor', None, 'seq'), may hold values from -0.09375 to 0.09375
- up_w: bfloat16 [4096, 3, 11008], P('tensor', None, 'seq'), may hold values from -0.09375 to 0.09375
- down_weight_matrix: bfloat16 [3, 11008, 4096], P(None, 'seq', 'tensor'), may hold values from -0.0546875 to 0.0546875
Outputs:
- layer_out: bfloat16 [1024, 4096], P('seq', 'tensor')
The draws below stay inside these ranges and needn't reach their ends.
Inputs may be any that keep to these rules, and one draw needn't show every extreme that they name: `modality`: in each shard of 128 consecutive tokens, at most 48 tokens carry any one tag; in every draw some shard has exactly 48 tokens with tag 0.
All inputs are finite; a program needn't handle non-finite values.
Results may differ from the reference program's by a relative error of at most 0.018.
Values may be sent and summed in bfloat16 or wider, within the bound.
No kernel may reach another device: no remote copies, remote signals or barrier semaphores. Data moves between devices by JAX's collectives and lax.ppermute only.
A program may use at most 128 MiB of HBM per device.

```python
import math
import jax
import jax.numpy as jnp
import numpy as np
from jax import lax

D = 4096
HEADS = 32
FF = 11008
DH = 128
MODS = 3
DOCS = 4
TOK_DEV = 128
TOKENS = 1024
CAP = 48
N_TENSOR = 4


def query_key_pair(key):
    base = jax.random.fold_in(key, 9)
    key_query, key_keys = jax.random.split(base, 2)
    query_draw = jnp.clip(jax.random.normal(key_query, (TOKENS, D), jnp.float32), -6.0, 6.0)
    key_draw = jnp.clip(jax.random.normal(key_keys, (TOKENS, D), jnp.float32), -6.0, 6.0)
    return (query_draw, key_draw)


def draw_queries(key, part):
    return query_key_pair(key)[0].astype(jnp.bfloat16)


def draw_keys(key, part):
    return query_key_pair(key)[1].astype(jnp.bfloat16)


def draw_resid(key, part):
    base = jax.random.fold_in(key, 3)
    key_normal, key_column = jax.random.split(base, 2)
    entries = jnp.clip(jax.random.normal(key_normal, (TOKENS, D), jnp.float32), -5.0, 5.0)
    ramp = jnp.arange(D, dtype=jnp.float32) / D
    jitter = jax.random.uniform(key_column, (D,), minval=0.5, maxval=1.5)
    columns = 0.3 * 3.0 ** ramp * jitter
    return (entries * columns[None, :]).astype(jnp.bfloat16)


def draw_modality(key, part):
    base = jax.random.fold_in(key, 11)
    key_text, key_image, key_full, key_perm = jax.random.split(base, 4)
    shards = TOKENS // TOK_DEV
    text_low = max(0, TOK_DEV - 2 * CAP)
    text_count = jax.random.randint(key_text, (shards,), text_low, CAP + 1)
    full_shard = jax.random.randint(key_full, (), 0, shards)
    text_count = jnp.where(jnp.arange(shards, dtype=jnp.int32) == full_shard, CAP, text_count)
    remaining = TOK_DEV - text_count
    lowest = jnp.maximum(0, remaining - CAP)
    highest = jnp.minimum(CAP, remaining)
    image_count = lowest + jax.random.randint(key_image, (shards,), 0, 1 << 20) % (highest - lowest + 1)
    slot_index = jnp.arange(TOK_DEV, dtype=jnp.int32)[None, :]
    ordered = jnp.where(slot_index < text_count[:, None], 0, jnp.where(slot_index < (text_count + image_count)[:, None], 1, 2)).astype(jnp.int32)
    perm_keys = jax.random.split(key_perm, shards)
    orders = jax.vmap(lambda one_key: jax.random.permutation(one_key, TOK_DEV))(perm_keys)
    shuffled = jnp.take_along_axis(ordered, orders, axis=1)
    return shuffled.reshape(TOKENS).astype(jnp.int32)


def block_scale(own_key, dims, cuts, least, largest):
    gain, own = 1.0, jax.random.fold_in(own_key, 6)
    for dim, shards_of in cuts:
        heights = jnp.exp(jax.random.uniform(jax.random.fold_in(own, dim), (shards_of,), jnp.float32, least / len(cuts), largest / len(cuts)))
        gain = gain * jnp.repeat(heights, dims[dim] // shards_of).reshape([-1 if axis == dim else 1 for axis in range(len(dims))])
    return gain


def length_profile(number_of, total, most, skew):
    weights = [(1 << 20) // math.isqrt(standing ** skew) + 1 for standing in range(2, number_of + 1)]
    rest, given = total - most - (number_of - 1), [1] * (number_of - 1)
    while rest > 0:
        movable = [i for i in range(number_of - 1) if given[i] < most]
        whole, left = sum([weights[i] for i in movable]), rest
        for i in movable:
            more = min(most - given[i], max(1, left * weights[i] // whole), rest)
            given[i] = given[i] + more
            rest = rest - more
    return np.array([most] + given)


def ragged_sizes(stream_key, number_of, total, most, slope):
    if number_of == 2:
        one = jax.random.randint(stream_key, (), max(1, total - most), min(most, total - 1) + 1)
        return jnp.stack([one, total - one])
    sizes = jnp.asarray(length_profile(number_of, total, most, slope), jnp.int32)
    twos = (number_of - 1) // 2
    source_of, sink = sizes[1:1 + 2 * twos:2], sizes[2:2 + 2 * twos:2]
    margin = jnp.minimum(source_of - 1, most - sink)
    moved = jax.random.randint(jax.random.fold_in(stream_key, 1), (twos,), 0, 1 << 20) % (margin + 1)
    sizes = sizes.at[1:1 + 2 * twos:2].set(source_of - moved).at[2:2 + 2 * twos:2].set(sink + moved)
    return sizes[jax.random.permutation(jax.random.fold_in(stream_key, 2), number_of)]


def normal_values(stream_key, extent, scale, reach, cuts=(), held_as=jnp.bfloat16):
    values = scale * jax.random.normal(stream_key, extent, jnp.float32)
    if cuts:
        values = values * block_scale(stream_key, extent, cuts, -0.22, 0.18)
    return jnp.clip(values, -reach, reach).astype(held_as)


def setup_inputs(seed: int = 0) -> dict:
    arg_keys = jax.random.split(jax.random.key(seed), 11)
    resid = draw_resid(jax.random.fold_in(arg_keys[10], 71), 0)
    queries = draw_queries(jax.random.fold_in(arg_keys[10], 71), 0)
    keys = draw_keys(jax.random.fold_in(arg_keys[10], 71), 0)
    values = normal_values(arg_keys[3], (TOKENS, D), 3.0, 18.0, ((0, 8), (1, 4)))
    doc_ids = jnp.searchsorted(jnp.cumsum(ragged_sizes(arg_keys[4], DOCS, TOKENS, TOKENS // 2, 0)), jnp.arange(TOKENS), side="right").astype(jnp.int32)
    modality = draw_modality(jax.random.fold_in(arg_keys[10], 71), 0)
    norm_gain = jnp.clip(1.0 + 0.18 * jax.random.normal(arg_keys[6], (MODS, D), jnp.float32), 0.1, 1.9)
    gate_w = normal_values(arg_keys[7], (D, MODS, FF), D ** -0.5, 0.09375, ((0, 4), (2, 8)))
    up_w = normal_values(arg_keys[8], (D, MODS, FF), D ** -0.5, 0.09375, ((0, 4), (2, 8)))
    down_weight_matrix = normal_values(arg_keys[9], (MODS, FF, D), FF ** -0.5, 0.0546875, ((1, 8), (2, 4)))
    return dict(resid=resid, queries=queries, keys=keys, values=values, doc_ids=doc_ids, modality=modality, norm_gain=norm_gain, gate_w=gate_w, up_w=up_w, down_weight_matrix=down_weight_matrix)


def reference(resid, queries, keys, values, doc_ids, modality, norm_gain, gate_w, up_w, down_weight_matrix):
    positions = jnp.arange(TOKENS, dtype=jnp.int32)
    allowed = (positions[None, :] <= positions[:, None]) & (doc_ids[None, :] == doc_ids[:, None])
    scale_factor = 1.0 / math.sqrt(DH)

    def head_attend(operands):
        q_head, k_head, v_head = operands
        scores = jnp.dot(q_head, k_head.T, preferred_element_type=jnp.float32) * scale_factor
        scores = jnp.where(allowed, scores, -1e+30)
        row_max = lax.optimization_barrier(jnp.max(scores, axis=1, keepdims=True))
        powers = jnp.where(allowed, jnp.exp(scores - row_max), 0.0)
        totals = lax.optimization_barrier(jnp.sum(powers, axis=1, keepdims=True))
        blended = jnp.dot(powers.astype(jnp.bfloat16), v_head, preferred_element_type=jnp.float32)
        return blended / totals

    def split_heads(matrix):
        return matrix.reshape(TOKENS, HEADS, DH).transpose(1, 0, 2)
    per_head = lax.map(head_attend, (split_heads(queries), split_heads(keys), split_heads(values)))
    attended = per_head.transpose(1, 0, 2).reshape(TOKENS, D).astype(jnp.bfloat16)
    stream = resid.astype(jnp.float32) + attended.astype(jnp.float32)
    inv_rms = lax.rsqrt(lax.optimization_barrier(jnp.mean(stream * stream, axis=1, keepdims=True)) + 1e-05)
    normalized_input = (stream * inv_rms * norm_gain[modality]).astype(jnp.bfloat16)
    shards = TOKENS // TOK_DEV
    tag_rows = modality.reshape(shards, TOK_DEV)
    onehot = (tag_rows[:, :, None] == jnp.arange(3, dtype=jnp.int32)[None, None, :]).astype(jnp.int32)
    slot_rank = lax.optimization_barrier(jnp.sum(onehot * (jnp.cumsum(onehot, axis=1) - 1), axis=2))
    normed_rows = normalized_input.reshape(shards, TOK_DEV, D).astype(jnp.float32)
    block_width = D // N_TENSOR
    ffn_sum = jnp.zeros((shards, TOK_DEV, D), jnp.float32)
    for served in range(MODS):
        placing = ((tag_rows == served)[:, None, :] & (slot_rank[:, None, :] == jnp.arange(CAP, dtype=jnp.int32)[None, :, None])).astype(jnp.float32)
        buffer = jnp.einsum('scr,srf->scf', placing, normed_rows, precision=lax.Precision.HIGHEST)
        buffer = buffer.astype(jnp.bfloat16).reshape(shards * CAP, D)
        gate_slab = gate_w[:, served, :]
        up_weight_block = up_w[:, served, :]
        down_slab = down_weight_matrix[served]

        def add_block(block_index, running):
            offset = (block_index * block_width).astype(jnp.int32)
            inputs = lax.dynamic_slice_in_dim(buffer, offset, block_width, 1)
            gate_rows = lax.dynamic_slice_in_dim(gate_slab, offset, block_width, 0)
            up_rows = lax.dynamic_slice_in_dim(up_weight_block, offset, block_width, 0)
            gate_piece = jnp.dot(inputs, gate_rows, preferred_element_type=jnp.float32).astype(jnp.bfloat16)
            up_piece = jnp.dot(inputs, up_rows, preferred_element_type=jnp.float32).astype(jnp.bfloat16)
            gate_piece, up_piece = lax.optimization_barrier((gate_piece, up_piece))
            return (running[0] + gate_piece.astype(jnp.float32), running[1] + up_piece.astype(jnp.float32))
        empty_total = jnp.zeros((shards * CAP, FF), jnp.float32)
        gate_sum, up_sum = lax.fori_loop(0, N_TENSOR, add_block, (empty_total, empty_total))
        hidden = (jax.nn.silu(gate_sum) * up_sum).astype(jnp.bfloat16)
        slot_part = jnp.dot(hidden, down_slab, preferred_element_type=jnp.float32).reshape(shards, CAP, D)
        ffn_sum = ffn_sum + jnp.einsum('scr,scf->srf', placing, slot_part, precision=lax.Precision.HIGHEST)
    return (stream + ffn_sum.reshape(TOKENS, D)).astype(jnp.bfloat16)
```

```python
import functools
import math

import jax
import jax.numpy as jnp
from jax import lax
from jax.experimental import pallas as pl
from jax.experimental.pallas import tpu as pltpu
from jax.sharding import PartitionSpec as P

D = 4096
DH = 128
MODS = 3
CAP = 48
CORES = 2
NT_DIMS = (((1,), (1,)), ((), ()))
NN_DIMS = (((1,), (0,)), ((), ()))
BF16 = jnp.bfloat16
F32 = jnp.float32


def attend_kernel(count, q_ref, *refs):
    k_refs, v_refs = refs[:count], refs[count : 2 * count]
    bias_ref, resid_ref, gain_ref, onehot_ref, placing_ref = refs[2 * count : 2 * count + 5]
    stream_ref, squares_ref = refs[2 * count + 5 : 2 * count + 7]
    slot_refs = refs[2 * count + 7 :]
    scale = 1.0 / math.sqrt(DH)
    outs = []
    for head in range(q_ref.shape[1] // DH):
        cols = slice(head * DH, (head + 1) * DH)
        keys = jnp.concatenate([ref[:, cols] for ref in k_refs], axis=0)
        vals = jnp.concatenate([ref[:, cols] for ref in v_refs], axis=0)
        scores = lax.dot_general(q_ref[:, cols], keys, NT_DIMS, preferred_element_type=F32)
        scores = scores * scale + bias_ref[...]
        powers = jnp.exp(scores - jnp.max(scores, axis=1, keepdims=True))
        total = jnp.sum(powers, axis=1, keepdims=True)
        blended = lax.dot_general(powers.astype(BF16), vals, NN_DIMS, preferred_element_type=F32)
        outs.append((blended / total).astype(BF16).astype(F32))
    stream = resid_ref[...].astype(F32) + jnp.concatenate(outs, axis=1)
    stream_ref[...] = stream

    @pl.when(pl.program_id(0) == 0)
    def _():
        squares_ref[...] = jnp.zeros_like(squares_ref)

    squares_ref[...] += jnp.sum(stream * stream, axis=1, keepdims=True)
    gain = sum(onehot_ref[:, m : m + 1] * gain_ref[m : m + 1, :] for m in range(MODS))
    scaled = (stream * gain).astype(BF16)
    slots = lax.dot_general(placing_ref[...], scaled, NN_DIMS, preferred_element_type=F32)
    slots = slots.astype(BF16)
    for m, ref in enumerate(slot_refs):
        ref[...] = slots[m * CAP : (m + 1) * CAP]


def attend(queries, keys, values, bias, resid, norm_gain, onehot, placing):
    rows, feats = queries.shape
    wide = min(2 * DH, feats)
    column = pl.BlockSpec((rows, wide), lambda i: (0, i))
    whole = lambda a: pl.BlockSpec(a.shape, lambda i: (0, 0))
    count = len(keys)
    return pl.pallas_call(
        functools.partial(attend_kernel, count),
        grid=(feats // wide,),
        in_specs=[column] * (1 + 2 * count)
        + [whole(bias), column, pl.BlockSpec((MODS, wide), lambda i: (0, i)), whole(onehot), whole(placing)],
        out_specs=[column, pl.BlockSpec((rows, 1), lambda i: (0, 0))]
        + [pl.BlockSpec((CAP, wide), lambda i: (0, i))] * MODS,
        out_shape=[jax.ShapeDtypeStruct((rows, feats), F32), jax.ShapeDtypeStruct((rows, 1), F32)]
        + [jax.ShapeDtypeStruct((CAP, feats), BF16)] * MODS,
        cost_estimate=pl.CostEstimate(
            flops=4 * rows * rows * count * feats,
            bytes_accessed=2 * rows * feats * 2 * count,
            transcendentals=rows * rows * count * feats // DH,
        ),
        name="attend",
    )(queries, *keys, *values, bias, resid, norm_gain, onehot, placing)


def gate_up_kernel(pieces, core_ref, *refs):
    piece_refs = refs[:pieces]
    gate_ref, up_ref, keep_ref, send_ref, rows_ref = refs[pieces:]
    half = pieces // CORES

    @pl.when(pl.program_id(0) == 0)
    def _():
        for p, ref in enumerate(piece_refs):
            away = jnp.where(core_ref[0] == p % CORES, 0, half)
            start = pl.multiple_of((away + p // CORES) * CAP, CAP)
            rows_ref[pl.ds(start, CAP), :] = ref[...]

    for which, w_ref in enumerate((gate_ref, up_ref)):
        product = lax.dot_general(rows_ref[...], w_ref[0], NT_DIMS, preferred_element_type=F32)
        product = product.astype(BF16)
        for p in range(half):
            keep_ref[which, p] = product[p * CAP : (p + 1) * CAP]
            send_ref[which, p] = product[(half + p) * CAP : (half + p + 1) * CAP]


def gate_up(core, pieces, gate_w, up_w, m):
    _, units, feats = gate_w.shape
    count = len(pieces)
    half = count // CORES
    block = min(512, units)
    weight = pl.BlockSpec((1, block, feats), lambda i, _: (m, i, 0))
    result = pl.BlockSpec((2, half, CAP, block), lambda i, _: (0, 0, 0, i))
    shape = jax.ShapeDtypeStruct((2, half, CAP, units), BF16)
    return pl.pallas_call(
        functools.partial(gate_up_kernel, count),
        grid_spec=pltpu.PrefetchScalarGridSpec(
            num_scalar_prefetch=1,
            grid=(pl.cdiv(units, block),),
            in_specs=[pl.BlockSpec((CAP, feats), lambda i, _: (0, 0))] * count + [weight, weight],
            out_specs=[result, result],
            scratch_shapes=[pltpu.VMEM((count * CAP, feats), BF16)],
        ),
        out_shape=[shape, shape],
        cost_estimate=pl.CostEstimate(
            flops=4 * count * CAP * feats * units,
            bytes_accessed=4 * feats * units + 2 * count * CAP * (feats + 2 * units),
            transcendentals=0,
        ),
        name="gate_up",
    )(core, *pieces, gate_w, up_w)


def down_kernel(pieces, across, place_ref, *refs):
    hidden_refs = refs[:pieces]
    w_ref, *out_refs, rows_ref = refs[pieces:]

    @pl.when(pl.program_id(0) == 0)
    def _():
        for p, ref in enumerate(hidden_refs):
            start = pl.multiple_of(place_ref[p] * CAP, CAP)
            rows_ref[pl.ds(start, CAP), :] = ref[...]

    product = lax.dot_general(rows_ref[...], w_ref[0], NN_DIMS, preferred_element_type=F32)
    deep = pieces // across
    for j, ref in enumerate(out_refs):
        for k in range(deep):
            at = j * deep + k
            ref[k] = product[at * CAP : (at + 1) * CAP].astype(ref.dtype)


def down(place, hidden, down_w, m, across):
    _, units, feats = down_w.shape
    count = len(hidden)
    deep = count // across
    block = min(512, feats)
    return pl.pallas_call(
        functools.partial(down_kernel, count, across),
        grid_spec=pltpu.PrefetchScalarGridSpec(
            num_scalar_prefetch=1,
            grid=(feats // block,),
            in_specs=[pl.BlockSpec((CAP, units), lambda i, _: (0, 0))] * count
            + [pl.BlockSpec((1, units, block), lambda i, _: (m, 0, i))],
            out_specs=[pl.BlockSpec((deep, CAP, block), lambda i, _: (0, 0, i))] * across,
            scratch_shapes=[pltpu.VMEM((count * CAP, units), BF16)],
        ),
        out_shape=[
            jax.ShapeDtypeStruct((deep, CAP, feats), BF16 if j else F32) for j in range(across)
        ],
        cost_estimate=pl.CostEstimate(
            flops=2 * count * CAP * feats * units,
            bytes_accessed=2 * feats * units + 2 * count * CAP * (feats + units),
            transcendentals=0,
        ),
        name="down",
    )(place, *hidden, down_w)


def finish_kernel(stream_ref, spread_ref, *refs):
    part_refs, out_ref = refs[:-1], refs[-1]
    parts = jnp.concatenate([ref[...] for ref in part_refs], axis=0)
    high = parts.astype(BF16)
    low = (parts - high.astype(F32)).astype(BF16)
    spread = spread_ref[...]
    ffn = lax.dot_general(spread, high, NN_DIMS, preferred_element_type=F32)
    ffn += lax.dot_general(spread, low, NN_DIMS, preferred_element_type=F32)
    out_ref[...] = (stream_ref[...] + ffn).astype(BF16)


def finish(stream, spread, parts):
    return pl.pallas_call(
        finish_kernel, out_shape=jax.ShapeDtypeStruct(stream.shape, BF16), name="finish"
    )(stream, spread, *parts)


def on_device(
    resid, queries, keys, values, doc_ids, modality, norm_gain, gate_w, up_w, down_weight_matrix
):
    rows, feats = resid.shape
    ns, nt = lax.axis_size("seq"), lax.axis_size("tensor")
    nx = math.isqrt(ns // 2)
    nz, ny = ns // nx, nt // CORES
    assert nx * nz == ns and ny * CORES == nt and nt % nx == 0 and ns % nt == 0
    assert not (nx & (nx - 1) or nz & (nz - 1) or ny & (ny - 1))
    s, t = lax.axis_index("seq"), lax.axis_index("tensor")
    z, x = s // nx, s % nx
    y, core = t // CORES, t % CORES

    def swap_seq(a, step, keep=lambda here, there: True):
        return lax.ppermute(
            a, "seq", [(i, i ^ step) for i in range(ns) if keep(i % nx, (i ^ step) % nx)]
        )

    def swap_z(a, k):
        return swap_seq(a, k * nx)

    def swap_tensor(a, step):
        return lax.ppermute(a, "tensor", [(i, i ^ step) for i in range(nt)])

    def forward(a, step):
        return lax.ppermute(a, "seq", [(i, i + step) for i in range(ns - step)])

    back = nz // 2
    window = back * nx
    longest = window * rows
    k_rows, v_rows = [keys], [values]
    k_all, v_all, bases = [], [], []
    for r in range(back + 1):
        if r:
            k_rows.append(forward(k_rows[-1], nx))
            v_rows.append(forward(v_rows[-1], nx))
        for j in range(nx):
            if j == 0:
                k_all.append(k_rows[r])
                v_all.append(v_rows[r])
            else:
                if r == 0:
                    keep = lambda here, there: here < there
                elif r == back:
                    keep = lambda here, there: here > there
                else:
                    keep = lambda here, there: True
                k_all.append(swap_seq(k_rows[r], j, keep))
                v_all.append(swap_seq(v_rows[r], j, keep))
            bases.append(((z - r) * nx + (x ^ j)) * rows)

    marks = (doc_ids + 1).reshape(1, rows)
    own = marks.reshape(rows, 1)
    earlier = jnp.concatenate([forward(marks, i + 1) for i in range(window)], axis=1)
    begin = (
        s * rows
        + jnp.sum((marks < own).astype(jnp.int32), axis=1, keepdims=True)
        - jnp.sum((earlier == own).astype(jnp.int32), axis=1, keepdims=True)
    )
    query_pos = s * rows + jnp.arange(rows, dtype=jnp.int32)[:, None]
    begin = jnp.maximum(begin, query_pos - longest + 1)
    key_pos = jnp.concatenate([b + jnp.arange(rows, dtype=jnp.int32) for b in bases])[None, :]
    allowed = (key_pos <= query_pos) & (key_pos >= begin)
    bias = jnp.where(allowed, 0.0, -1e30).astype(F32)

    onehot = (modality[:, None] == jnp.arange(MODS, dtype=jnp.int32)[None, :]).astype(F32)
    slot_rank = jnp.sum(onehot * (jnp.cumsum(onehot, axis=0) - 1.0), axis=1)
    slot_grid = jnp.arange(CAP, dtype=F32)
    placing = onehot.T[:, None, :] * (slot_rank[None, None, :] == slot_grid[None, :, None])
    placing = placing.astype(F32).reshape(MODS * CAP, rows)

    stream, squares, *slots = attend(
        queries, k_all, v_all, bias, resid, norm_gain, onehot, placing.astype(BF16)
    )

    slot_squares = jnp.sum(placing * squares.reshape(1, rows), axis=1).reshape(MODS, CAP)
    by_z = [[m] if k == 0 else [swap_z(v, k) for v in m] for k in range(nz) for m in [slots]]
    by_z[0] = slots
    pieces = []
    for k in range(nz):
        for j in range(nx):
            pieces.append([swap_seq(v, j) for v in by_z[k]] if j else by_z[k])
    sq_z = [swap_z(slot_squares, k) if k else slot_squares for k in range(nz)]
    sq = jnp.stack([swap_seq(v, j) if j else v for v in sq_z for j in range(nx)])
    for step in [CORES * k for k in range(1, ny)]:
        pass
    total_sq = sq + swap_tensor(sq, 1)
    total_sq = total_sq + sum(swap_tensor(total_sq, CORES * k) for k in range(1, ny))
    inv_rms = lax.rsqrt(total_sq / D + 1e-05)

    gate_t, up_t = gate_w.transpose(1, 2, 0), up_w.transpose(1, 2, 0)
    deep = nt // nx
    core_arg = core.reshape(1).astype(jnp.int32)
    ys = [0] + [CORES * k for k in range(1, ny)]
    arrivals = [step ^ c for c in range(CORES) for step in ys]
    owners = jnp.stack([t ^ a for a in arrivals]).astype(jnp.int32)
    place = (owners % nx) * deep + owners // nx

    ffn = [None] * MODS
    for g in range(ns // nt):
        group = pieces[g * nt : (g + 1) * nt]
        for m in range(MODS):
            keep, send = gate_up(core_arg, [p[m] for p in group], gate_t, up_t, m)
            got = swap_tensor(send, 1)

            def row_of(index):
                take = lambda a: lax.dynamic_index_in_dim(a, index, 1, keepdims=False)
                return take(keep).astype(F32) + take(got).astype(F32)

            total = row_of(y)
            for k in range(1, ny):
                total = total + swap_tensor(row_of(y ^ k).astype(BF16), CORES * k).astype(F32)
            inv = lax.dynamic_index_in_dim(inv_rms[:, m], g * nt + t, 0, keepdims=False)[:, None]
            gate, up = total[0] * inv, total[1] * inv
            share = (gate / (1.0 + jnp.exp(-gate)) * up).astype(BF16)
            hidden = [share] + [swap_tensor(share, step) for step in ys[1:]]
            hidden = hidden + [swap_tensor(h, 1) for h in hidden]
            parts = down(place, hidden, down_weight_matrix, m, nx)
            total = parts[0]
            for j in range(1, nx):
                total = total + swap_seq(parts[j], j).astype(F32)
            for k in range(deep):
                far = g * deep + k
                part = swap_z(total[k].astype(BF16), far).astype(F32) if far else total[k]
                ffn[m] = part if ffn[m] is None else ffn[m] + part

    return finish(stream, placing.T.astype(BF16), ffn)


def solution(mesh):
    in_specs = (
        P("seq", "tensor"),
        P("seq", "tensor"),
        P("seq", "tensor"),
        P("seq", "tensor"),
        P("seq"),
        P("seq"),
        P(None, "tensor"),
        P("tensor", None, "seq"),
        P("tensor", None, "seq"),
        P(None, "seq", "tensor"),
    )
    out_specs = P("seq", "tensor")
    return jax.shard_map(
        on_device, mesh=mesh, in_specs=in_specs, out_specs=out_specs, check_vma=False
    )
```
